32 devices in a mesh: face: 4 (over x, core), tile: 8 (over z, y).
Axes of the slice: x: 2, y: 2, z: 4, core: 2. Of those that a mesh axis runs over, the one named last changes fastest.
Arguments:
- pressure: float32 [64, 512, 256], P(None, ('face', 'tile')), may hold values from -0.8 to 0.8
- forcing: float32 [64, 512, 256], P(None, ('face', 'tile')), may hold values from -8 to 8
- stiffness: float32 [64, 512, 256], P(None, ('face', 'tile')), may hold values from 2 to 8
- vertical_op: float32 [64, 64], replicated, as said below
- col_inverse: float32 [4, 64, 64], replicated, as said below
Outputs:
- updated: float32 [64, 512, 256], P(None, ('face', 'tile'))
- new_residual: float32 [64, 512, 256], P(None, ('face', 'tile'))
The draws below stay inside these ranges and needn't reach their ends.
Inputs may be any that keep to these rules, and one draw needn't show every extreme that they name: vertical_op is symmetric positive definite. col_inverse[l] is the float32 inverse of (0.02 + 16 / 4^l) I + vertical_op.
All inputs are finite; a program needn't handle non-finite values.
Results may differ from the reference program's by a relative error of at most 0.0003.
Values sent between devices are 32-bit elements; how exact they have to be, the bound alone decides.
No kernel may reach another device: no remote copies, remote signals or barrier semaphores. Data moves between devices by JAX's collectives and lax.ppermute only.
A program may use at most 128 MiB of HBM per device.

```python
import math
import jax
import jax.numpy as jnp
from jax import lax

LEV = 64
CY = 256
LEVELS = 4
COARSE_SWEEPS = 4
NX = 512


def vertical_pair(key):
    folded = jax.random.fold_in(key, 7)
    coef_key, jitter_key = jax.random.split(folded)
    interfaces = jnp.exp(jax.random.uniform(coef_key, (LEV + 1,), jnp.float32, 0.0, jnp.log(8.0)))
    identity = jnp.eye(LEV, dtype=jnp.float32)
    diag_part = interfaces[:-1] + interfaces[1:] + 0.3
    off_diag = -interfaces[1:-1]
    tridiag = jnp.diag(diag_part) + jnp.diag(off_diag, 1) + jnp.diag(off_diag, -1)
    jitter = jax.random.normal(jitter_key, (LEV, LEV), jnp.float32) * 0.01
    operator = tridiag + (jitter + jitter.T) * 0.7071
    inverses = jnp.stack([jnp.linalg.inv((0.02 + 16.0 / 4.0 ** grid_level) * identity + operator) for grid_level in range(LEVELS)])
    return (operator, inverses)


def draw_vertical_op(key, part):
    return vertical_pair(key)[0]


def draw_col_inverse(key, part):
    return vertical_pair(key)[1]


def steps_of(key, dims, shards, least, largest):
    loudness, own = 1.0, jax.random.fold_in(key, 6)
    for axis_at, shards_of in shards:
        steps = jnp.exp(jax.random.uniform(jax.random.fold_in(own, axis_at), (shards_of,), jnp.float32, least / len(shards), largest / len(shards)))
        loudness = loudness * jnp.repeat(steps, dims[axis_at] // shards_of).reshape([-1 if axis == axis_at else 1 for axis in range(len(dims))])
    return loudness


def bell_draw(rng, extent, width, reach, pieces=(), held_as=jnp.bfloat16):
    drawn = jax.random.normal(rng, extent, jnp.float32) * width
    if len(pieces) > 0:
        drawn = steps_of(rng, extent, pieces, -0.22, 0.18) * drawn
    return jnp.clip(drawn, min=-reach, max=reach).astype(held_as)


def setup_inputs(seed: int = 0) -> dict:
    key_of = jax.random.split(jax.random.key(seed), 6)
    return {
        "pressure": bell_draw(key_of[0], (LEV, NX, CY), 0.1, 0.8, ((1, 32),), jnp.float32),
        "forcing": bell_draw(key_of[1], (LEV, NX, CY), 1.0, 8.0, ((1, 32),), jnp.float32),
        "stiffness": jnp.clip(jnp.exp(math.log(8.0) - 1.3862944 * jax.random.uniform(key_of[2], (LEV, NX, CY), jnp.float32) ** steps_of(key_of[2], (LEV, NX, CY), ((1, 32),), -0.2, 0.2)), 2.0, 8.0),
        "vertical_op": draw_vertical_op(jax.random.fold_in(key_of[5], 71), 0),
        "col_inverse": draw_col_inverse(jax.random.fold_in(key_of[5], 71), 0),
    }


damping = 0.02
relax_weight = 0.6
nominal_stiff = 16.0

def column_apply(matrix, values):
    flattened = values.reshape(values.shape[0], -1)
    return jnp.dot(matrix.astype(jnp.float32), flattened.astype(jnp.float32), precision=lax.Precision.HIGHEST, preferred_element_type=jnp.float32).reshape(values.shape)

def lateral_sum(values):
    zero_col = jnp.zeros_like(values[:, :, :1])
    upward = jnp.concatenate([values[:, :, 1:], zero_col], axis=2)
    downward = jnp.concatenate([zero_col, values[:, :, :-1]], axis=2)
    return upward + downward

def operator_from(values, beside_sum, stiffness, vertical_op):
    horizontal = stiffness * (4.0 * values - beside_sum - lateral_sum(values))
    return damping * values + horizontal + column_apply(vertical_op, values)

def loop_operator(values, stiffness, vertical_op):
    beside_sum = jnp.roll(values, 1, 1) + jnp.roll(values, -1, 1)
    return operator_from(values, beside_sum, stiffness, vertical_op)

def coarsen(values):
    return values.reshape(values.shape[0], values.shape[1] // 2, 2, values.shape[2] // 2, 2).mean(axis=(2, 4))

def refine(values):
    return jnp.repeat(jnp.repeat(values, 2, axis=1), 2, axis=2)

def relax_step(correction, source, scaling, matrix, operator):
    return correction + relax_weight * column_apply(matrix, scaling * (source - operator(correction)))

def vcycle(source, stiffness, vertical_op, col_inverse, grid_level):
    scaling = (damping + nominal_stiff / 4.0 ** grid_level) / (damping + 4.0 * stiffness)
    matrix = col_inverse[grid_level]

    def operator(values):
        return loop_operator(values, stiffness, vertical_op)
    correction = relax_weight * column_apply(matrix, scaling * source)
    if grid_level == LEVELS - 1:
        for sweep_index in range(COARSE_SWEEPS - 1):
            correction = relax_step(correction, source, scaling, matrix, operator)
        return correction
    correction = relax_step(correction, source, scaling, matrix, operator)
    residue = source - operator(correction)
    coarse_fix = vcycle(coarsen(residue), coarsen(stiffness) / 4.0, vertical_op, col_inverse, grid_level + 1)
    correction = correction + refine(coarse_fix)
    for sweep_index in range(2):
        correction = relax_step(correction, source, scaling, matrix, operator)
    return correction

def reference(pressure, forcing, stiffness, vertical_op, col_inverse):
    start_res = forcing - loop_operator(pressure, stiffness, vertical_op)
    updated = pressure + vcycle(start_res, stiffness, vertical_op, col_inverse, 0)
    return (updated, forcing - loop_operator(updated, stiffness, vertical_op))
```

```python
import functools

import jax
import jax.numpy as jnp
from jax import lax
from jax.experimental import pallas as pl
from jax.experimental.pallas import tpu as pltpu
from jax.sharding import PartitionSpec as P

AXES = ("face", "tile")
LANES = 128
damping = 0.02
relax_weight = 0.6
nominal_stiff = 16.0
F32 = jnp.float32
BF16 = jnp.bfloat16


def nominal(level):
    return nominal_stiff / 4.0**level


def halves(x):
    hi = x.astype(BF16)
    return hi, (x - hi.astype(F32)).astype(BF16)


def column_matrix(m):
    hi = m.astype(BF16).astype(F32)
    lo = m - hi
    return jnp.concatenate([hi, hi, lo], axis=1).astype(BF16)


def column_apply(m3, t):
    z = m3.shape[0]
    out = []
    for i in range(t.shape[0] // z):
        hi, lo = halves(t[i * z : (i + 1) * z])
        out.append(
            jnp.dot(m3, jnp.concatenate([hi, lo, hi], axis=0), preferred_element_type=F32)
        )
    return out[0] if len(out) == 1 else jnp.concatenate(out, axis=0)


def lane_matrix(lanes_in, lanes_out, value, spread):
    i = lax.broadcasted_iota(jnp.int32, (lanes_in, lanes_out), 0)
    j = lax.broadcasted_iota(jnp.int32, (lanes_in, lanes_out), 1)
    hit = (j // 2 == i) if spread else (i // 2 == j)
    one = jnp.where(hit, F32(value), F32(0.0))
    return jnp.concatenate([one, one], axis=0).astype(BF16)


def lane_apply(v, m2):
    hi, lo = halves(v)
    return jnp.dot(jnp.concatenate([hi, lo], axis=1), m2, preferred_element_type=F32)


def side_rows(v, valid):
    lanes = v.shape[1]
    north = pltpu.roll(v, 1, 1)
    south = pltpu.roll(v, lanes - 1, 1)
    if valid == lanes:
        lane = lax.broadcasted_iota(jnp.int32, v.shape, 1)
        north = jnp.where(lane == 0, 0.0, north)
        south = jnp.where(lane == lanes - 1, 0.0, south)
    return north + south


def lap(west, mid, east, valid):
    return 4.0 * mid - (west + east) - side_rows(mid, valid)


def scaling(k, level):
    return (relax_weight * (damping + nominal(level))) / (damping + 4.0 * k)


def packed(blocks, valid):
    out = blocks[0]
    for i, v in enumerate(blocks[1:], 1):
        out = out + pltpu.roll(v, i * valid, 1)
    return out


def unpacked(v, i, valid):
    v = v if i == 0 else pltpu.roll(v, LANES - i * valid, 1)
    lane = lax.broadcasted_iota(jnp.int32, v.shape, 1)
    return jnp.where(lane < valid, v, 0.0)


def over(lo, hi, unroll, body):
    full = (hi - lo) // unroll
    if full > 1:
        lax.fori_loop(0, full, lambda i, _: (body(lo + i * unroll, unroll), 0)[1], 0)
    elif full == 1:
        body(lo, unroll)
    if (hi - lo) % unroll:
        body(lo + full * unroll, (hi - lo) % unroll)


class Field:
    def __init__(self, ref, z, halo):
        self.ref, self.z, self.halo = ref, z, halo

    def at(self, pos, n=1):
        start = (pos + self.halo) * self.z
        if not isinstance(start, int):
            start = pl.multiple_of(start, self.z)
        return pl.ds(start, n * self.z)

    def get(self, pos, n=1):
        return self.ref[self.at(pos, n), :]

    def put(self, pos, v, n=1):
        self.ref[self.at(pos, n), :] = v


def operator_part(r, d, k, s, level, valid, pos, n):
    rv, mid = r.get(pos, n), d.get(pos, n)
    sides = lap(d.get(pos - 1, n), mid, d.get(pos + 1, n), valid)
    return rv - (s.get(pos, n) * rv + k.get(pos, n) * sides - nominal(level) * mid)


def sweep(r, d, nxt, k, s, m3, level, valid, lo, hi, unroll):
    def body(pos, n):
        rv = operator_part(r, d, k, s, level, valid, pos, n)
        r.put(pos, rv, n)
        nxt.put(pos, column_apply(m3, s.get(pos, n) * rv), n)

    over(lo, hi, unroll, body)


def residue(r, d, k, s, level, valid, lo, hi, unroll):
    def body(pos, n):
        r.put(pos, operator_part(r, d, k, s, level, valid, pos, n), n)

    over(lo, hi, unroll, body)


def coarsen(fine, coarse, matrix, lo, hi):
    for pos in range(lo, hi):
        coarse.put(pos, lane_apply(fine.get(2 * pos) + fine.get(2 * pos + 1), matrix))


def refine(e, v3, spread, d, g, lo, hi):
    for pos in range(lo, hi):
        ev = e.get(pos)
        dv = lane_apply(ev, spread)
        gv = lane_apply(damping * ev + column_apply(v3, ev), spread)
        for i in (0, 1):
            d.put(2 * pos + i, dv)
            g.put(2 * pos + i, gv)


def after_coarse(r, d, g, nxt, k, s, m3, valid, lo, hi, unroll):
    def body(pos, n):
        sides = lap(d.get(pos - 1, n), d.get(pos, n), d.get(pos + 1, n), valid)
        rv = r.get(pos, n) - (k.get(pos, n) * sides + g.get(pos, n))
        r.put(pos, rv, n)
        nxt.put(pos, column_apply(m3, s.get(pos, n) * rv), n)

    over(lo, hi, unroll, body)


VM = pl.BlockSpec(memory_space=pltpu.VMEM)
ANY = pl.BlockSpec(memory_space=pl.ANY)


def lane_halves(ref, buf, sems, inward):
    out = []
    for i in range(2):
        far, near = ref.at[:, pl.ds(i * LANES, LANES)], buf.at[i]
        src, dst = (far, near) if inward else (near, far)
        out.append(pltpu.make_async_copy(src, dst, sems.at[i]))
    return out


def block_rows(buf, pos, z, n):
    rows = pl.ds(pos, z, stride=n)
    return jnp.concatenate([buf[0, rows, :], buf[1, rows, :]], axis=1)


def put_block_rows(buf, pos, z, n, v):
    rows = pl.ds(pos, z, stride=n)
    for i in range(2):
        buf[i, rows, :] = v[:, i * LANES : (i + 1) * LANES]


def kernel_call(fn, outs, scratch, args, aliases=None, far_in=0, far_out=0, sems=()):
    return pl.pallas_call(
        fn,
        out_shape=[jax.ShapeDtypeStruct(o, F32) for o in outs],
        in_specs=[ANY] * far_in + [VM] * (len(args) - far_in),
        out_specs=[VM] * (len(outs) - far_out) + [ANY] * far_out,
        scratch_shapes=[pltpu.VMEM(s, F32) for s in scratch]
        + [pltpu.SemaphoreType.DMA((n,)) for n in sems],
        input_output_aliases=aliases or {},
        name=fn.__name__,
        compiler_params=pltpu.CompilerParams(vmem_limit_bytes=40 * 1024 * 1024),
    )(*args)


def body(devices, pressure, forcing, stiffness, vertical_op, col_inverse):
    z, n0, r0 = pressure.shape
    pos = [n0 >> lev for lev in range(4)]
    valid = [r0 >> lev for lev in range(4)]
    lanes = [max(LANES, v) for v in valid]
    n1, n2, n3 = pos[1:]
    halo = [2, 4, 4, 5]
    span = [(pos[lev] + 2 * halo[lev]) * z for lev in range(4)]
    ext = [(span[lev], lanes[lev]) for lev in range(4)]
    own = [(pos[lev] * z, lanes[lev]) for lev in range(4)]

    def right(v, d=1):
        return lax.ppermute(v, AXES, [(i, (i + d) % devices) for i in range(devices)])

    def left(v, d=1):
        return lax.ppermute(v, AXES, [(i, (i - d) % devices) for i in range(devices)])

    flat = [v.reshape(z * n0, r0) for v in (pressure, forcing, stiffness)]

    def edges_of(i):
        return jnp.concatenate([pressure[:, i, :], stiffness[:, i, :]], axis=0)

    first, last = edges_of(0), edges_of(n0 - 1)
    pk_from_right, pk_from_left = left(first), right(last)

    def start_kernel(
        p, f, k, v, c, ke, se, re, de, to_left, to_right, pb, kbuf, pbuf, fbuf, ksem, psem, fsem
    ):
        copies = [
            lane_halves(far, buf, sem, True)
            for far, buf, sem in ((k, kbuf, ksem), (p, pbuf, psem), (f, fbuf, fsem))
        ]
        for pair in copies:
            for copy in pair:
                copy.start()
        ke, se, re, de = (Field(x, z, halo[0]) for x in (ke, se, re, de))
        pb = Field(pb, z, 1)
        m3 = column_matrix(c[0])
        v3 = column_matrix(v[...])
        pb.put(-1, jnp.zeros((z, r0), F32))
        pb.put(n0, jnp.zeros((z, r0), F32))

        for pair in copies[:2]:
            for copy in pair:
                copy.wait()

        def load(i, n):
            for j in range(n):
                kv = block_rows(kbuf, i + j, z, n0)
                ke.put(i + j, kv)
                se.put(i + j, scaling(kv, 0))
                pb.put(i + j, block_rows(pbuf, i + j, z, n0))

        over(0, n0, 4, load)

        for copy in copies[2]:
            copy.wait()

        def start(i, n):
            for j in range(n):
                q = i + j
                mid = pb.get(q)
                sides = lap(pb.get(q - 1), mid, pb.get(q + 1), valid[0])
                rv = block_rows(fbuf, q, z, n0) - (
                    damping * mid + ke.get(q) * sides + column_apply(v3, mid)
                )
                re.put(q, rv)
                de.put(q, column_apply(m3, se.get(q) * rv))

        over(0, n0, 4, start)
        for out, q, step in ((to_left, 0, 1), (to_right, n0 - 1, -1)):
            out[:z, :] = re.get(q)
            out[z:, :] = de.get(q + step)

    k_ext, s_ext, r_ext, d_ext, rd_left, rd_right = kernel_call(
        start_kernel,
        [ext[0]] * 4 + [(2 * z, r0)] * 2,
        [((n0 + 2) * z, r0)] + [(2, z * n0, LANES)] * 3,
        [*flat, vertical_op, col_inverse],
        far_in=3,
        sems=(2, 2, 2),
    )
    rd_from_right, rd_from_left = left(rd_left), right(rd_right)

    def stiff_kernel(ke, k1, k2, k3, to_left, to_right):
        ke = Field(ke, z, halo[0])
        ks = [ke] + [Field(x, z, 0) for x in (k1, k2, k3)]
        for lev in range(3):
            matrix = lane_matrix(lanes[lev], lanes[lev + 1], 1.0 / 16.0, False)
            coarsen(ks[lev], ks[lev + 1], matrix, 0, pos[lev + 1])
        for out, at in ((to_left, lambda i, n: i), (to_right, lambda i, n: n - 1 - i)):
            out = Field(out, z, 0)
            k01 = ke.get(at(1, n0))
            out.put(0, k01[:, :LANES])
            out.put(1, k01[:, LANES:])
            for i in range(3):
                out.put(2 + i, ks[1].get(at(i, n1)))
            for i in range(2):
                out.put(5 + i, packed([ks[2].get(2 * i + j) for j in range(2)], valid[2]))

    k1, k2, k3, ks_left, ks_right = kernel_call(
        stiff_kernel, own[1:] + [(7 * z, LANES)] * 2, [], [k_ext]
    )
    ks_from_right, ks_from_left = left(ks_left), right(ks_right)

    def fine_kernel(
        first, last, pk_l, pk_r, rd_l, rd_r, k1, c, ke_i, se_i, re_i, de_i,
        ke, se, re, de, c0, b1, d1, to_left, to_right, r_left, r_right, d2
    ):
        ke, se, re, de, d2 = (Field(x, z, halo[0]) for x in (ke, se, re, de, d2))
        m3 = column_matrix(c[0])
        for mine, pk, rd, q, step in (
            (first, pk_l, rd_l, 0, -1),
            (last, pk_r, rd_r, n0 - 1, 1),
        ):
            h = q + step
            kh = pk[z:, :]
            ke.put(h, kh)
            se.put(h, scaling(kh, 0))
            re.put(h, rd[:z, :] + kh * mine[:z, :])
            re.put(q, re.get(q) + ke.get(q) * pk[:z, :])
            for at in (h, q):
                de.put(at, column_apply(m3, se.get(at) * re.get(at)))
            de.put(h + step, rd[z:, :])
        sweep(re, de, d2, ke, se, m3, 0, valid[0], -1, n0 + 1, 3)
        residue(re, d2, ke, se, 0, valid[0], 0, n0, 2)
        c0 = Field(c0, z, 0)
        over(0, n0, 4, lambda i, n: c0.put(i, de.get(i, n) + d2.get(i, n), n))
        b1 = Field(b1, z, halo[1])
        coarsen(re, b1, lane_matrix(lanes[0], lanes[1], 0.25, False), 0, n1)
        d1 = Field(d1, z, halo[1])
        k1 = Field(k1, z, 0)
        m1 = column_matrix(c[1])
        for i in range(n1):
            d1.put(i, column_apply(m1, scaling(k1.get(i), 1) * b1.get(i)))
        for out, q, step in ((to_left, 0, 1), (to_right, n1 - 1, -1)):
            out[:z, :] = b1.get(q)
            out[z:, :] = d1.get(q + step)
        for out, q, step in ((r_left, 0, 1), (r_right, n0 - 1, -1)):
            out[:z, :] = re.get(q)
            out[z:, :] = re.get(q + step)

    k_ext, s_ext, r_ext, d_ext, c0, b1, d1, bd_left, bd_right, r_left, r_right = kernel_call(
        fine_kernel,
        [ext[0]] * 4 + [own[0], ext[1], ext[1]] + [(2 * z, lanes[1])] * 2 + [(2 * z, r0)] * 2,
        [ext[0]],
        [first, last, pk_from_left, pk_from_right, rd_from_left, rd_from_right, k1, col_inverse,
         k_ext, s_ext, r_ext, d_ext],
        {8: 0, 9: 1, 10: 2, 11: 3},
    )
    bd_from_right, bd_from_left = left(bd_left), right(bd_right)
    r_from_right, r_from_left = left(r_left), right(r_right)

    def second_kernel(
        bd_l, bd_r, ks_l, ks_r, k1_i, k2_i, c, b1_i, d1_i,
        b1, d1, k1, s1, b2, to_left, to_right, m_left, m_right, d2
    ):
        b1, d1, k1, s1, d2 = (Field(x, z, halo[1]) for x in (b1, d1, k1, s1, d2))
        b2 = Field(b2, z, halo[2])
        k1_i = Field(k1_i, z, 0)
        m3 = column_matrix(c[1])
        k1.put(0, k1_i.get(0, n1), n1)
        for ks, bd, q, step in ((ks_l, bd_l, -1, -1), (ks_r, bd_r, n1, 1)):
            ks = Field(ks, z, 0)
            for i in range(3):
                k1.put(q + i * step, ks.get(2 + i))
            b1.put(q, bd[:z, :])
            d1.put(q + step, bd[z:, :])
        over(-3, n1 + 3, 7, lambda i, n: s1.put(i, scaling(k1.get(i, n), 1), n))
        for q in (-1, n1):
            d1.put(q, column_apply(m3, s1.get(q) * b1.get(q)))
        sweep(b1, d1, d2, k1, s1, m3, 1, valid[1], -1, n1 + 1, 5)
        residue(b1, d2, k1, s1, 1, valid[1], 0, n1, 4)
        coarsen(b1, b2, lane_matrix(lanes[1], lanes[2], 0.25, False), 0, n2)
        for i in range(2):
            both = packed([b2.get(2 * i + j) for j in range(2)], valid[2])
            for out in (to_left, to_right):
                out[i * z : (i + 1) * z, :] = both
        for out, q, step in ((m_left, 0, 1), (m_right, n1 - 1, -1)):
            out = Field(out, z, 0)
            for i in range(3):
                out.put(i, b1.get(q + i * step))
            out.put(3, d2.get(q + step))
        d1.put(-1, d1.get(-1, n1 + 2) + d2.get(-1, n1 + 2), n1 + 2)

    r1, c1, k1e, s1e, b2, b2_left, b2_right, m_left, m_right = kernel_call(
        second_kernel,
        [ext[1]] * 4 + [ext[2]] + [(n2 // 2 * z, LANES)] * 2 + [(4 * z, LANES)] * 2,
        [ext[1]],
        [bd_from_left, bd_from_right, ks_from_left, ks_from_right, k1, k2, col_inverse, b1, d1],
        {7: 0, 8: 1},
    )
    b2_from_right, b2_from_left = left(b2_left), right(b2_right)
    m_from_right, m_from_left = left(m_left), right(m_right)

    def third_kernel(
        b2_l, b2_r, ks_l, ks_r, k2_i, c, b2_i, b2, d1, k2, s2, w3, to_left, to_right, d2
    ):
        b2, d1, k2, s2, d2 = (Field(x, z, halo[2]) for x in (b2, d1, k2, s2, d2))
        k2_i = Field(k2_i, z, 0)
        m3 = column_matrix(c[2])
        k2.put(0, k2_i.get(0, n2), n2)
        for ks, b, base in ((ks_l, b2_l, -n2), (ks_r, b2_r, n2)):
            ks, b = Field(ks, z, 0), Field(b, z, 0)
            for i in range(n2):
                b2.put(base + i, unpacked(b.get(i // 2), i % 2, valid[2]))
                k2.put(base + i, unpacked(ks.get(5 + i // 2), i % 2, valid[2]))
        for i in range(-n2, 2 * n2):
            s2.put(i, scaling(k2.get(i), 2))
            d1.put(i, column_apply(m3, s2.get(i) * b2.get(i)))
        sweep(b2, d1, d2, k2, s2, m3, 2, valid[2], -3, n2 + 3, 5)
        residue(b2, d2, k2, s2, 2, valid[2], -2, n2 + 2, 4)
        w3 = Field(w3, z, 0)
        for src, to, value in ((b2, 0, 0.25), (k2, 1, 1.0 / 16.0)):
            matrix = lane_matrix(lanes[2], lanes[3], value, False)
            rows = [
                lane_apply(src.get(2 * i) + src.get(2 * i + 1), matrix)
                for i in range(-1, n3 + 1)
            ]
            w3.put(to, packed(rows, valid[3]))
        for out, q in ((to_left, -2), (to_right, n2 + 1)):
            out = Field(out, z, 0)
            out.put(0, w3.get(0))
            out.put(1, w3.get(1))
            out.put(2, b2.get(q))
        d1.put(-2, d1.get(-2, n2 + 4) + d2.get(-2, n2 + 4), n2 + 4)

    r2, c2, k2e, s2e, w3, w_left, w_right = kernel_call(
        third_kernel,
        [ext[2]] * 4 + [(2 * z, LANES)] + [(3 * z, LANES)] * 2,
        [ext[2]],
        [b2_from_left, b2_from_right, ks_from_left, ks_from_right, k2, col_inverse, b2],
        {6: 0},
    )
    w_from_right, w_from_left = left(w_left, 2), right(w_right, 2)

    def coarse_kernel(w_l, w_r, w, c, v, c2, k2, s2, r2_i, r2, e2, b3, k3, s3, da, db, e3, d3, g3, d4, d5):
        b3, k3, s3, da, db, e3 = (Field(x, z, halo[3]) for x in (b3, k3, s3, da, db, e3))
        c2, k2, s2, r2, e2, d3, g3, d4, d5 = (
            Field(x, z, halo[2]) for x in (c2, k2, s2, r2, e2, d3, g3, d4, d5)
        )
        m3 = column_matrix(c[3])
        v3 = column_matrix(v[...])
        for src, base in ((w_l, -5), (w, -1), (w_r, 3)):
            src = Field(src, z, 0)
            bv, kv = src.get(0), src.get(1)
            for i in range(4):
                b3.put(base + i, unpacked(bv, i, valid[3]))
                k3.put(base + i, unpacked(kv, i, valid[3]))
        for i in range(-5, n3 + 5):
            s3.put(i, scaling(k3.get(i), 3))
            da.put(i, column_apply(m3, s3.get(i) * b3.get(i)))
        e3.put(-2, da.get(-2, n3 + 4), n3 + 4)
        for reach in (4, 3, 2):
            sweep(b3, da, db, k3, s3, m3, 3, valid[3], -reach, n3 + reach, 5)
            e3.put(-2, e3.get(-2, n3 + 4) + db.get(-2, n3 + 4), n3 + 4)
            da, db = db, da
        r2.put(-3, Field(w_l, z, 0).get(2))
        r2.put(n2 + 2, Field(w_r, z, 0).get(2))
        m2 = column_matrix(c[2])
        refine(e3, v3, lane_matrix(lanes[3], lanes[2], 1.0, True), d3, g3, -2, n3 + 2)
        after_coarse(r2, d3, g3, d4, k2, s2, m2, valid[2], -3, n2 + 3, 5)
        sweep(r2, d4, d5, k2, s2, m2, 2, valid[2], -2, n2 + 2, 4)
        q, m = -2, n2 + 4
        e2.put(q, c2.get(q, m) + d3.get(q, m) + d4.get(q, m) + d5.get(q, m), m)

    _, e2 = kernel_call(
        coarse_kernel,
        [ext[2]] * 2,
        [ext[3]] * 6 + [ext[2]] * 4,
        [w_from_left, w_from_right, w3, col_inverse, vertical_op, c2, k2e, s2e, r2],
        {8: 0},
    )

    def second_up_kernel(m_l, m_r, c, v, e2, k1, s1, c1, r1_i, r1, e1, d3, g3, d4, d5):
        e2 = Field(e2, z, halo[2])
        k1, s1, c1, r1, e1, d3, g3, d4, d5 = (
            Field(x, z, halo[1]) for x in (k1, s1, c1, r1, e1, d3, g3, d4, d5)
        )
        m1 = column_matrix(c[1])
        v3 = column_matrix(v[...])
        for m, q, step in ((m_l, -1, -1), (m_r, n1, 1)):
            m = Field(m, z, 0)
            for i in range(3):
                r1.put(q + i * step, m.get(i))
        refine(e2, v3, lane_matrix(lanes[2], lanes[1], 1.0, True), d3, g3, -2, n2 + 2)
        after_coarse(r1, d3, g3, d4, k1, s1, m1, valid[1], -3, n1 + 3, 7)
        sweep(r1, d4, d5, k1, s1, m1, 1, valid[1], -2, n1 + 2, 6)
        q, n = -2, n1 + 4
        e1.put(q, c1.get(q, n) + d3.get(q, n) + d4.get(q, n) + d5.get(q, n), n)
        for m, at in ((m_l, -2), (m_r, n1 + 1)):
            e1.put(at, e1.get(at) + Field(m, z, 0).get(3))

    _, e1 = kernel_call(
        second_up_kernel,
        [ext[1]] * 2,
        [ext[1]] * 4,
        [m_from_left, m_from_right, col_inverse, vertical_op, e2, k1e, s1e, c1, r1],
        {8: 0},
    )

    def last_kernel(
        p, r_l, r_r, ks_l, ks_r, c, v, e1, c0, ke_i, se_i, re_i,
        ke, se, re, up, res, d3, g3, d4, d5, pbuf, ubuf, vbuf, psem, usem, vsem
    ):
        loads = lane_halves(p, pbuf, psem, True)
        for copy in loads:
            copy.start()
        e1 = Field(e1, z, halo[1])
        ke, se, re, d4, d5 = (Field(x, z, halo[0]) for x in (ke, se, re, d4, d5))
        d3, g3 = (Field(x, z, 4) for x in (d3, g3))
        c0 = Field(c0, z, 0)
        m3 = column_matrix(c[0])
        v3 = column_matrix(v[...])
        for r, ks, q, step in ((r_l, ks_l, -1, -1), (r_r, ks_r, n0, 1)):
            re.put(q, r[:z, :])
            re.put(q + step, r[z:, :])
            ks = Field(ks, z, 0)
            kv = jnp.concatenate([ks.get(0), ks.get(1)], axis=1)
            ke.put(q + step, kv)
            se.put(q + step, scaling(kv, 0))
        refine(e1, v3, lane_matrix(lanes[1], lanes[0], 1.0, True), d3, g3, -2, n1 + 2)
        after_coarse(re, d3, g3, d4, ke, se, m3, valid[0], -2, n0 + 2, 4)
        sweep(re, d4, d5, ke, se, m3, 0, valid[0], -1, n0 + 1, 3)

        for copy in loads:
            copy.wait()

        def total(i, n):
            for j in range(n):
                q = i + j
                c = c0.get(q) + d3.get(q) + d4.get(q) + d5.get(q)
                put_block_rows(ubuf, q, z, n0, block_rows(pbuf, q, z, n0) + c)

        over(0, n0, 4, total)
        stores = lane_halves(up, ubuf, usem, False)
        for copy in stores:
            copy.start()

        def finish(i, n):
            for j in range(n):
                q = i + j
                rv = operator_part(re, d5, ke, se, 0, valid[0], q, 1)
                put_block_rows(vbuf, q, z, n0, rv)

        over(0, n0, 4, finish)
        more = lane_halves(res, vbuf, vsem, False)
        for copy in more:
            copy.start()
        for copy in stores + more:
            copy.wait()

    outs = kernel_call(
        last_kernel,
        [ext[0]] * 3 + [(z * n0, r0)] * 2,
        [((n0 + 8) * z, r0)] * 2 + [ext[0]] * 2 + [(2, z * n0, LANES)] * 3,
        [flat[0], r_from_left, r_from_right, ks_from_left, ks_from_right, col_inverse, vertical_op,
         e1, c0, k_ext, s_ext, r_ext],
        {9: 0, 10: 1, 11: 2},
        far_in=1,
        far_out=2,
        sems=(2, 2, 2),
    )
    return tuple(o.reshape(z, n0, r0) for o in outs[3:])


def solution(mesh):
    devices = 1
    for axis in AXES:
        devices *= mesh.shape[axis]
    split = P(None, AXES, None)
    return jax.shard_map(
        functools.partial(body, devices),
        mesh=mesh,
        in_specs=(split, split, split, P(), P()),
        out_specs=(split, split),
        check_vma=False,
    )
```

```python
import functools

import jax
import jax.numpy as jnp
from jax import lax
from jax.experimental import pallas as pl
from jax.experimental.pallas import tpu as pltpu
from jax.sharding import PartitionSpec as P

AXES = ("face", "tile")
LANES = 128
damping = 0.02
relax_weight = 0.6
nominal_stiff = 16.0
F32 = jnp.float32
BF16 = jnp.bfloat16


def nominal(level):
    return nominal_stiff / 4.0**level


def halves(x):
    hi = x.astype(BF16)
    return hi, (x - hi.astype(F32)).astype(BF16)


def column_matrix(m):
    hi = m.astype(BF16).astype(F32)
    lo = m - hi
    return jnp.concatenate([hi, hi, lo], axis=1).astype(BF16)


def column_apply(m3, t):
    z = m3.shape[0]
    out = []
    for i in range(t.shape[0] // z):
        hi, lo = halves(t[i * z : (i + 1) * z])
        out.append(
            jnp.dot(m3, jnp.concatenate([hi, lo, hi], axis=0), preferred_element_type=F32)
        )
    return out[0] if len(out) == 1 else jnp.concatenate(out, axis=0)


def lane_matrix(lanes_in, lanes_out, value, spread):
    i = lax.broadcasted_iota(jnp.int32, (lanes_in, lanes_out), 0)
    j = lax.broadcasted_iota(jnp.int32, (lanes_in, lanes_out), 1)
    hit = (j // 2 == i) if spread else (i // 2 == j)
    one = jnp.where(hit, F32(value), F32(0.0))
    return jnp.concatenate([one, one], axis=0).astype(BF16)


def lane_apply(v, m2):
    hi, lo = halves(v)
    return jnp.dot(jnp.concatenate([hi, lo], axis=1), m2, preferred_element_type=F32)


def side_rows(v, valid):
    lanes = v.shape[1]
    north = pltpu.roll(v, 1, 1)
    south = pltpu.roll(v, lanes - 1, 1)
    if valid == lanes:
        lane = lax.broadcasted_iota(jnp.int32, v.shape, 1)
        north = jnp.where(lane == 0, 0.0, north)
        south = jnp.where(lane == lanes - 1, 0.0, south)
    return north + south


def lap(west, mid, east, valid):
    return 4.0 * mid - (west + east) - side_rows(mid, valid)


def scaling(k, level):
    return (relax_weight * (damping + nominal(level))) / (damping + 4.0 * k)


def packed(blocks, valid):
    out = blocks[0]
    for i, v in enumerate(blocks[1:], 1):
        out = out + pltpu.roll(v, i * valid, 1)
    return out


def unpacked(v, i, valid):
    v = v if i == 0 else pltpu.roll(v, LANES - i * valid, 1)
    lane = lax.broadcasted_iota(jnp.int32, v.shape, 1)
    return jnp.where(lane < valid, v, 0.0)


def over(lo, hi, unroll, body):
    full = (hi - lo) // unroll
    if full > 1:
        lax.fori_loop(0, full, lambda i, _: (body(lo + i * unroll, unroll), 0)[1], 0)
    elif full == 1:
        body(lo, unroll)
    if (hi - lo) % unroll:
        body(lo + full * unroll, (hi - lo) % unroll)


class Field:
    def __init__(self, ref, z, halo):
        self.ref, self.z, self.halo = ref, z, halo

    def at(self, pos, n=1):
        start = (pos + self.halo) * self.z
        if not isinstance(start, int):
            start = pl.multiple_of(start, self.z)
        return pl.ds(start, n * self.z)

    def get(self, pos, n=1):
        return self.ref[self.at(pos, n), :]

    def put(self, pos, v, n=1):
        self.ref[self.at(pos, n), :] = v


def operator_part(r, d, k, s, level, valid, pos, n):
    rv, mid = r.get(pos, n), d.get(pos, n)
    sides = lap(d.get(pos - 1, n), mid, d.get(pos + 1, n), valid)
    return rv - (s.get(pos, n) * rv + k.get(pos, n) * sides - nominal(level) * mid)


def sweep(r, d, nxt, k, s, m3, level, valid, lo, hi, unroll):
    def body(pos, n):
        rv = operator_part(r, d, k, s, level, valid, pos, n)
        r.put(pos, rv, n)
        nxt.put(pos, column_apply(m3, s.get(pos, n) * rv), n)

    over(lo, hi, unroll, body)


def residue(r, d, k, s, level, valid, lo, hi, unroll):
    def body(pos, n):
        r.put(pos, operator_part(r, d, k, s, level, valid, pos, n), n)

    over(lo, hi, unroll, body)


def coarsen(fine, coarse, matrix, lo, hi):
    for pos in range(lo, hi):
        coarse.put(pos, lane_apply(fine.get(2 * pos) + fine.get(2 * pos + 1), matrix))


def refine(e, v3, spread, d, g, lo, hi):
    for pos in range(lo, hi):
        ev = e.get(pos)
        dv = lane_apply(ev, spread)
        gv = lane_apply(damping * ev + column_apply(v3, ev), spread)
        for i in (0, 1):
            d.put(2 * pos + i, dv)
            g.put(2 * pos + i, gv)


def after_coarse(r, d, g, nxt, k, s, m3, valid, lo, hi, unroll):
    def body(pos, n):
        sides = lap(d.get(pos - 1, n), d.get(pos, n), d.get(pos + 1, n), valid)
        rv = r.get(pos, n) - (k.get(pos, n) * sides + g.get(pos, n))
        r.put(pos, rv, n)
        nxt.put(pos, column_apply(m3, s.get(pos, n) * rv), n)

    over(lo, hi, unroll, body)


VM = pl.BlockSpec(memory_space=pltpu.VMEM)
ANY = pl.BlockSpec(memory_space=pltpu.HBM)


def lane_halves(ref, buf, sems, inward):
    out = []
    for i in range(2):
        far, near = ref.at[:, pl.ds(i * LANES, LANES)], buf.at[i]
        src, dst = (far, near) if inward else (near, far)
        out.append(pltpu.make_async_copy(src, dst, sems.at[i]))
    return out


def block_rows(buf, pos, z, n):
    rows = pl.ds(pos, z, stride=n)
    return jnp.concatenate([buf[0, rows, :], buf[1, rows, :]], axis=1)


def put_block_rows(buf, pos, z, n, v):
    rows = pl.ds(pos, z, stride=n)
    for i in range(2):
        buf[i, rows, :] = v[:, i * LANES : (i + 1) * LANES]


def kernel_call(fn, outs, scratch, args, aliases=None, far_in=0, far_out=0, sems=()):
    return pl.pallas_call(
        fn,
        out_shape=[jax.ShapeDtypeStruct(o, F32) for o in outs],
        in_specs=[ANY] * far_in + [VM] * (len(args) - far_in),
        out_specs=[VM] * (len(outs) - far_out) + [ANY] * far_out,
        scratch_shapes=[pltpu.VMEM(s, F32) for s in scratch]
        + [pltpu.SemaphoreType.DMA((n,)) for n in sems],
        input_output_aliases=aliases or {},
        name=fn.__name__,
        compiler_params=pltpu.CompilerParams(vmem_limit_bytes=40 * 1024 * 1024),
    )(*args)


def body(devices, pressure, forcing, stiffness, vertical_op, col_inverse):
    z, n0, r0 = pressure.shape
    pos = [n0 >> lev for lev in range(4)]
    valid = [r0 >> lev for lev in range(4)]
    lanes = [max(LANES, v) for v in valid]
    n1, n2, n3 = pos[1:]
    halo = [2, 4, 4, 5]
    span = [(pos[lev] + 2 * halo[lev]) * z for lev in range(4)]
    ext = [(span[lev], lanes[lev]) for lev in range(4)]
    own = [(pos[lev] * z, lanes[lev]) for lev in range(4)]

    def swap(v, d, odd):
        pairs = []
        for i in range(devices):
            up = (i // d + odd) % 2 == 0
            pairs.append((i, (i + (d if up else -d)) % devices))
        return lax.ppermute(v, AXES, pairs)

    def exchange(odd_side, even_side, d=1):
        return swap(odd_side, d, 1), swap(even_side, d, 0)

    def low_first(d=1):
        return 1 - lax.rem(lax.axis_index(AXES[1]) // d, 2)

    def inner(n, first):
        edge = (1 - first) * (n - 1)
        return ((edge, 2 * first - 1), ((n - 1) - edge, 1 - 2 * first))

    def outer(n, first):
        edge = n - first * (n + 1)
        return ((edge, 1 - 2 * first), ((n - 1) - edge, 2 * first - 1))

    flat = [v.reshape(z * n0, r0) for v in (pressure, forcing, stiffness)]

    def start_kernel(
        p, f, k, v, c, ke, se, re, de, to_o, to_e, pb, kbuf, pbuf, fbuf, ksem, psem, fsem
    ):
        copies = [
            lane_halves(far, buf, sem, True)
            for far, buf, sem in ((k, kbuf, ksem), (p, pbuf, psem), (f, fbuf, fsem))
        ]
        for pair in copies:
            for copy in pair:
                copy.start()
        ke, se, re, de = (Field(x, z, halo[0]) for x in (ke, se, re, de))
        pb = Field(pb, z, 1)
        m3 = column_matrix(c[0])
        v3 = column_matrix(v[...])
        pb.put(-1, jnp.zeros((z, r0), F32))
        pb.put(n0, jnp.zeros((z, r0), F32))
        for pair in copies[:2]:
            for copy in pair:
                copy.wait()

        def load(i, n):
            for j in range(n):
                kv = block_rows(kbuf, i + j, z, n0)
                ke.put(i + j, kv)
                se.put(i + j, scaling(kv, 0))
                pb.put(i + j, block_rows(pbuf, i + j, z, n0))

        over(0, n0, 4, load)
        for copy in copies[2]:
            copy.wait()

        def start(i, n):
            for j in range(n):
                q = i + j
                mid = pb.get(q)
                sides = lap(pb.get(q - 1), mid, pb.get(q + 1), valid[0])
                rv = block_rows(fbuf, q, z, n0) - (
                    damping * mid + ke.get(q) * sides + column_apply(v3, mid)
                )
                re.put(q, rv)
                de.put(q, column_apply(m3, se.get(q) * rv))

        over(0, n0, 4, start)
        for out, (q, step) in zip((to_o, to_e), inner(n0, low_first())):
            out = Field(out, z, 0)
            for i, v in enumerate((pb.get(q), ke.get(q), re.get(q), de.get(q + step))):
                out.put(i, v)

    k_ext, s_ext, r_ext, d_ext, e_o, e_e = kernel_call(
        start_kernel,
        [ext[0]] * 4 + [(4 * z, r0)] * 2,
        [((n0 + 2) * z, r0)] + [(2, z * n0, LANES)] * 3,
        [*flat, vertical_op, col_inverse],
        far_in=3,
        sems=(2, 2, 2),
    )
    with jax.named_scope("edge"):
        from_o, from_e = exchange(e_o, e_e)

    def stiff_kernel(ke, k1, k2, k3, to_o, to_e):
        ke = Field(ke, z, halo[0])
        ks = [ke] + [Field(x, z, 0) for x in (k1, k2, k3)]
        for lev in range(3):
            matrix = lane_matrix(lanes[lev], lanes[lev + 1], 1.0 / 16.0, False)
            coarsen(ks[lev], ks[lev + 1], matrix, 0, pos[lev + 1])
        first = low_first()
        for out, (q, step), (q1, step1) in zip((to_o, to_e), inner(n0, first), inner(n1, first)):
            out = Field(out, z, 0)
            k01 = ke.get(q + step)
            out.put(0, k01[:, :LANES])
            out.put(1, k01[:, LANES:])
            for i in range(3):
                out.put(2 + i, ks[1].get(q1 + i * step1))
            for i in range(2):
                out.put(5 + i, packed([ks[2].get(2 * i + j) for j in range(2)], valid[2]))

    k1, k2, k3, ks_o, ks_e = kernel_call(
        stiff_kernel, own[1:] + [(7 * z, LANES)] * 2, [], [k_ext]
    )
    with jax.named_scope("stiff"):
        ks_from_o, ks_from_e = exchange(ks_o, ks_e)

    def inner_kernel(k1, c, ke, se, de, re_i, re, d2, c0, b1, d1):
        ke, se, re, de, d2 = (Field(x, z, halo[0]) for x in (ke, se, re, de, d2))
        re_i = Field(re_i, z, halo[0])
        c0, k1 = (Field(x, z, 0) for x in (c0, k1))
        b1, d1 = (Field(x, z, halo[1]) for x in (b1, d1))
        m3 = column_matrix(c[0])
        m1 = column_matrix(c[1])
        sweep(re, de, d2, ke, se, m3, 0, valid[0], 2, n0 - 2, 4)
        residue(re, d2, ke, se, 0, valid[0], 3, n0 - 3, 2)
        over(2, n0 - 2, 4, lambda i, n: c0.put(i, de.get(i, n) + d2.get(i, n), n))
        coarsen(re, b1, lane_matrix(lanes[0], lanes[1], 0.25, False), 2, n1 - 2)
        for i in range(2, n1 - 2):
            d1.put(i, column_apply(m1, scaling(k1.get(i), 1) * b1.get(i)))

    r_ext, d2_ext, c0, b1, d1 = kernel_call(
        inner_kernel,
        [ext[0]] * 2 + [own[0], ext[1], ext[1]],
        [],
        [k1, col_inverse, k_ext, s_ext, d_ext, r_ext],
        {5: 0},
    )

    def fine_kernel(
        e_o, e_e, m_o, m_e, k1, c, ke_i, se_i, re_i, de, d2_i, c0_i, b1_i, d1_i,
        ke, se, re, d2, c0, b1, d1, to_o, to_e, r_o, r_e
    ):
        ke, se, re, de, d2 = (Field(x, z, halo[0]) for x in (ke, se, re, de, d2))
        c0, k1 = (Field(x, z, 0) for x in (c0, k1))
        b1, d1 = (Field(x, z, halo[1]) for x in (b1, d1))
        m3 = column_matrix(c[0])
        m1 = column_matrix(c[1])
        first = low_first()
        d2.put(-2, jnp.zeros((z, r0), F32))
        for mine, got, (h, step) in zip((e_o, e_e), (m_o, m_e), outer(n0, first)):
            mine, got = Field(mine, z, 0), Field(got, z, 0)
            q = h - step
            kh = got.get(1)
            ke.put(h, kh)
            se.put(h, scaling(kh, 0))
            re.put(h, got.get(2) + kh * mine.get(0))
            re.put(q, mine.get(2) + mine.get(1) * got.get(0))
            de.put(h + step, got.get(3))
        for h, q in ((-1, 0), (n0, n0 - 1)):
            for at in (h, q):
                de.put(at, column_apply(m3, se.get(at) * re.get(at)))
        for q in (-1, n0 - 2):
            sweep(re, de, d2, ke, se, m3, 0, valid[0], q, q + 3, 3)
        for q in (0, n0 - 3):
            residue(re, d2, ke, se, 0, valid[0], q, q + 3, 3)
        for q in (0, n0 - 2):
            c0.put(q, de.get(q, 2) + d2.get(q, 2), 2)
        matrix = lane_matrix(lanes[0], lanes[1], 0.25, False)
        for q in (0, n1 - 2):
            coarsen(re, b1, matrix, q, q + 2)
            for i in (q, q + 1):
                d1.put(i, column_apply(m1, scaling(k1.get(i), 1) * b1.get(i)))
        for out, (q, step) in zip((to_o, to_e), inner(n1, first)):
            out[:z, :] = b1.get(q)
            out[z:, :] = d1.get(q + step)
        for out, (q, step) in zip((r_o, r_e), inner(n0, first)):
            out[:z, :] = re.get(q)
            out[z:, :] = re.get(q + step)

    def fine_edges(e_o, e_e, m_o, m_e, k1, c, ke_i, se_i, re_i, de_i, d2_i, c0_i, b1_i, d1_i,
                   ke, se, re, de, d2, c0, b1, d1, to_o, to_e, r_o, r_e):
        fine_kernel(e_o, e_e, m_o, m_e, k1, c, ke_i, se_i, re_i, de, d2_i, c0_i, b1_i, d1_i,
                    ke, se, re, d2, c0, b1, d1, to_o, to_e, r_o, r_e)

    k_ext, s_ext, r_ext, _, _, c0, b1, d1, bd_o, bd_e, r_o, r_e = kernel_call(
        fine_edges,
        [ext[0]] * 5 + [own[0], ext[1], ext[1]] + [(2 * z, lanes[1])] * 2 + [(2 * z, r0)] * 2,
        [],
        [e_o, e_e, from_o, from_e, k1, col_inverse,
         k_ext, s_ext, r_ext, d_ext, d2_ext, c0, b1, d1],
        {6: 0, 7: 1, 8: 2, 9: 3, 10: 4, 11: 5, 12: 6, 13: 7},
    )
    with jax.named_scope("second"):
        bd_from_o, bd_from_e = exchange(bd_o, bd_e)
    with jax.named_scope("res0"):
        r_from_o, r_from_e = exchange(r_o, r_e)

    def second_kernel(
        bd_o, bd_e, ks_o, ks_e, k1_i, k2_i, c, b1_i, d1_i,
        b1, d1, k1, s1, b2, to, m_o, m_e, d2
    ):
        b1, d1, k1, s1, d2 = (Field(x, z, halo[1]) for x in (b1, d1, k1, s1, d2))
        b2 = Field(b2, z, halo[2])
        k1_i = Field(k1_i, z, 0)
        m3 = column_matrix(c[1])
        first = low_first()
        k1.put(0, k1_i.get(0, n1), n1)
        for ks, bd, (q, step) in zip((ks_o, ks_e), (bd_o, bd_e), outer(n1, first)):
            ks = Field(ks, z, 0)
            for i in range(3):
                k1.put(q + i * step, ks.get(2 + i))
            b1.put(q, bd[:z, :])
            d1.put(q + step, bd[z:, :])
        over(-3, n1 + 3, 7, lambda i, n: s1.put(i, scaling(k1.get(i, n), 1), n))
        for q in (-1, n1):
            d1.put(q, column_apply(m3, s1.get(q) * b1.get(q)))
        sweep(b1, d1, d2, k1, s1, m3, 1, valid[1], -1, n1 + 1, 5)
        residue(b1, d2, k1, s1, 1, valid[1], 0, n1, 4)
        coarsen(b1, b2, lane_matrix(lanes[1], lanes[2], 0.25, False), 0, n2)
        for i in range(2):
            both = packed([b2.get(2 * i + j) for j in range(2)], valid[2])
            to[i * z : (i + 1) * z, :] = both
        for out, (q, step) in zip((m_o, m_e), inner(n1, first)):
            out = Field(out, z, 0)
            for i in range(3):
                out.put(i, b1.get(q + i * step))
            out.put(3, d2.get(q + step))
        d1.put(-1, d1.get(-1, n1 + 2) + d2.get(-1, n1 + 2), n1 + 2)

    r1, c1, k1e, s1e, b2, b2_own, m_o, m_e = kernel_call(
        second_kernel,
        [ext[1]] * 4 + [ext[2]] + [(n2 // 2 * z, LANES)] + [(4 * z, LANES)] * 2,
        [ext[1]],
        [bd_from_o, bd_from_e, ks_from_o, ks_from_e, k1, k2, col_inverse, b1, d1],
        {7: 0, 8: 1},
    )
    with jax.named_scope("third"):
        b2_from_o, b2_from_e = exchange(b2_own, b2_own)
    with jax.named_scope("res1"):
        m_from_o, m_from_e = exchange(m_o, m_e)

    def third_kernel(
        b2_o, b2_e, ks_o, ks_e, k2_i, c, b2_i, b2, d1, k2, s2, w3, to_o, to_e, d2
    ):
        b2, d1, k2, s2, d2 = (Field(x, z, halo[2]) for x in (b2, d1, k2, s2, d2))
        k2_i = Field(k2_i, z, 0)
        m3 = column_matrix(c[2])
        k2.put(0, k2_i.get(0, n2), n2)
        first = low_first()
        for ks, b, base in ((ks_o, b2_o, n2 - 2 * n2 * first), (ks_e, b2_e, 2 * n2 * first - n2)):
            ks, b = Field(ks, z, 0), Field(b, z, 0)
            for i in range(n2):
                b2.put(base + i, unpacked(b.get(i // 2), i % 2, valid[2]))
                k2.put(base + i, unpacked(ks.get(5 + i // 2), i % 2, valid[2]))
        for i in range(-n2, 2 * n2):
            s2.put(i, scaling(k2.get(i), 2))
            d1.put(i, column_apply(m3, s2.get(i) * b2.get(i)))
        sweep(b2, d1, d2, k2, s2, m3, 2, valid[2], -3, n2 + 3, 5)
        residue(b2, d2, k2, s2, 2, valid[2], -2, n2 + 2, 4)
        w3 = Field(w3, z, 0)
        for src, to, value in ((b2, 0, 0.25), (k2, 1, 1.0 / 16.0)):
            matrix = lane_matrix(lanes[2], lanes[3], value, False)
            rows = [
                lane_apply(src.get(2 * i) + src.get(2 * i + 1), matrix)
                for i in range(-1, n3 + 1)
            ]
            w3.put(to, packed(rows, valid[3]))
        for out, (q, step) in zip((to_o, to_e), outer(n2, low_first(2))):
            out = Field(out, z, 0)
            out.put(0, w3.get(0))
            out.put(1, w3.get(1))
            out.put(2, b2.get(q + step))
        d1.put(-2, d1.get(-2, n2 + 4) + d2.get(-2, n2 + 4), n2 + 4)

    r2, c2, k2e, s2e, w3, w_o, w_e = kernel_call(
        third_kernel,
        [ext[2]] * 4 + [(2 * z, LANES)] + [(3 * z, LANES)] * 2,
        [ext[2]],
        [b2_from_o, b2_from_e, ks_from_o, ks_from_e, k2, col_inverse, b2],
        {6: 0},
    )
    with jax.named_scope("coarse"):
        w_from_o, w_from_e = exchange(w_o, w_e, 2)

    def coarse_kernel(w_o, w_e, w, c, v, c2, k2, s2, r2_i, r2, e2, b3, k3, s3, da, db, e3, d3, g3, d4, d5):
        b3, k3, s3, da, db, e3 = (Field(x, z, halo[3]) for x in (b3, k3, s3, da, db, e3))
        c2, k2, s2, r2, e2, d3, g3, d4, d5 = (
            Field(x, z, halo[2]) for x in (c2, k2, s2, r2, e2, d3, g3, d4, d5)
        )
        m3 = column_matrix(c[3])
        v3 = column_matrix(v[...])
        first = low_first(2)
        for src, base in ((w_o, 3 - 8 * first), (w, -1), (w_e, 8 * first - 5)):
            src = Field(src, z, 0)
            bv, kv = src.get(0), src.get(1)
            for i in range(4):
                b3.put(base + i, unpacked(bv, i, valid[3]))
                k3.put(base + i, unpacked(kv, i, valid[3]))
        for i in range(-5, n3 + 5):
            s3.put(i, scaling(k3.get(i), 3))
            da.put(i, column_apply(m3, s3.get(i) * b3.get(i)))
        e3.put(-2, da.get(-2, n3 + 4), n3 + 4)
        for reach in (4, 3, 2):
            sweep(b3, da, db, k3, s3, m3, 3, valid[3], -reach, n3 + reach, 5)
            e3.put(-2, e3.get(-2, n3 + 4) + db.get(-2, n3 + 4), n3 + 4)
            da, db = db, da
        for src, (q, step) in zip((w_o, w_e), outer(n2, first)):
            r2.put(q + 2 * step, Field(src, z, 0).get(2))
        m2 = column_matrix(c[2])
        refine(e3, v3, lane_matrix(lanes[3], lanes[2], 1.0, True), d3, g3, -2, n3 + 2)
        after_coarse(r2, d3, g3, d4, k2, s2, m2, valid[2], -3, n2 + 3, 5)
        sweep(r2, d4, d5, k2, s2, m2, 2, valid[2], -2, n2 + 2, 4)
        q, m = -2, n2 + 4
        e2.put(q, c2.get(q, m) + d3.get(q, m) + d4.get(q, m) + d5.get(q, m), m)

    _, e2 = kernel_call(
        coarse_kernel,
        [ext[2]] * 2,
        [ext[3]] * 6 + [ext[2]] * 4,
        [w_from_o, w_from_e, w3, col_inverse, vertical_op, c2, k2e, s2e, r2],
        {8: 0},
    )

    def second_up_kernel(m_o, m_e, c, v, e2, k1, s1, c1, r1_i, r1, e1, d3, g3, d4, d5):
        e2 = Field(e2, z, halo[2])
        k1, s1, c1, r1, e1, d3, g3, d4, d5 = (
            Field(x, z, halo[1]) for x in (k1, s1, c1, r1, e1, d3, g3, d4, d5)
        )
        m1 = column_matrix(c[1])
        v3 = column_matrix(v[...])
        sides = tuple(zip((m_o, m_e), outer(n1, low_first())))
        for m, (q, step) in sides:
            for i in range(3):
                r1.put(q + i * step, Field(m, z, 0).get(i))
        refine(e2, v3, lane_matrix(lanes[2], lanes[1], 1.0, True), d3, g3, -2, n2 + 2)
        after_coarse(r1, d3, g3, d4, k1, s1, m1, valid[1], -3, n1 + 3, 7)
        sweep(r1, d4, d5, k1, s1, m1, 1, valid[1], -2, n1 + 2, 6)
        q, n = -2, n1 + 4
        e1.put(q, c1.get(q, n) + d3.get(q, n) + d4.get(q, n) + d5.get(q, n), n)
        for m, (q, step) in sides:
            e1.put(q + step, e1.get(q + step) + Field(m, z, 0).get(3))

    _, e1 = kernel_call(
        second_up_kernel,
        [ext[1]] * 2,
        [ext[1]] * 4,
        [m_from_o, m_from_e, col_inverse, vertical_op, e2, k1e, s1e, c1, r1],
        {8: 0},
    )

    def last_kernel(
        p, r_o, r_e, ks_o, ks_e, c, v, e1, c0, ke_i, se_i, re_i,
        ke, se, re, up, res, d3, g3, d4, d5, pbuf, ubuf, vbuf, psem, usem, vsem
    ):
        loads = lane_halves(p, pbuf, psem, True)
        for copy in loads:
            copy.start()
        e1 = Field(e1, z, halo[1])
        ke, se, re, d4, d5 = (Field(x, z, halo[0]) for x in (ke, se, re, d4, d5))
        d3, g3 = (Field(x, z, 4) for x in (d3, g3))
        c0 = Field(c0, z, 0)
        m3 = column_matrix(c[0])
        v3 = column_matrix(v[...])
        for r, ks, (q, step) in zip((r_o, r_e), (ks_o, ks_e), outer(n0, low_first())):
            re.put(q, r[:z, :])
            re.put(q + step, r[z:, :])
            ks = Field(ks, z, 0)
            kv = jnp.concatenate([ks.get(0), ks.get(1)], axis=1)
            ke.put(q + step, kv)
            se.put(q + step, scaling(kv, 0))
        refine(e1, v3, lane_matrix(lanes[1], lanes[0], 1.0, True), d3, g3, -2, n1 + 2)
        after_coarse(re, d3, g3, d4, ke, se, m3, valid[0], -2, n0 + 2, 4)
        sweep(re, d4, d5, ke, se, m3, 0, valid[0], -1, n0 + 1, 3)

        for copy in loads:
            copy.wait()

        def total(i, n):
            for j in range(n):
                q = i + j
                c = c0.get(q) + d3.get(q) + d4.get(q) + d5.get(q)
                put_block_rows(ubuf, q, z, n0, block_rows(pbuf, q, z, n0) + c)

        over(0, n0, 4, total)
        stores = lane_halves(up, ubuf, usem, False)
        for copy in stores:
            copy.start()

        def finish(i, n):
            for j in range(n):
                q = i + j
                rv = operator_part(re, d5, ke, se, 0, valid[0], q, 1)
                put_block_rows(vbuf, q, z, n0, rv)

        over(0, n0, 4, finish)
        more = lane_halves(res, vbuf, vsem, False)
        for copy in more:
            copy.start()
        for copy in stores + more:
            copy.wait()

    outs = kernel_call(
        last_kernel,
        [ext[0]] * 3 + [(z * n0, r0)] * 2,
        [((n0 + 8) * z, r0)] * 2 + [ext[0]] * 2 + [(2, z * n0, LANES)] * 3,
        [flat[0], r_from_o, r_from_e, ks_from_o, ks_from_e, col_inverse, vertical_op,
         e1, c0, k_ext, s_ext, r_ext],
        {9: 0, 10: 1, 11: 2},
        far_in=1,
        far_out=2,
        sems=(2, 2, 2),
    )
    return tuple(o.reshape(z, n0, r0) for o in outs[3:])


def solution(mesh):
    devices = 1
    for axis in AXES:
        devices *= mesh.shape[axis]
    split = P(None, AXES, None)
    return jax.shard_map(
        functools.partial(body, devices),
        mesh=mesh,
        in_specs=(split, split, split, P(), P()),
        out_specs=(split, split),
        check_vma=False,
    )
```
